32 devices in a mesh: groups: 2 (over y), expert: 8 (over z, core), sub: 2 (over x).
Axes of the slice: x: 2, y: 2, z: 4, core: 2. Of those that a mesh axis runs over, the one named last changes fastest.
Arguments:
- latent: bfloat16 [4096, 1024], P(('groups', 'expert', 'sub')), parts along dimension 0, may hold values from -6 to 6
- routes: int32 [4096, 4], P(('groups', 'expert', 'sub')), parts along dimension 0, may hold values from 0 to 7, all different within a row; in each aligned block of 128 rows (0 to 127, 128 to 255, ...) at most 96 rows name the same one
- gates: float32 [4096, 4], P(('groups', 'expert', 'sub')), parts along dimension 0, may hold values from 0.1 to 1
- up_weight: bfloat16 [8, 1024, 2688], P('expert', None, 'sub'), may hold values from -0.1875 to 0.1875
- down_weight: bfloat16 [8, 1024, 2688], P('expert', None, 'sub'), may hold values from -0.125 to 0.125
Outputs:
- mixed: bfloat16 [4096, 1024], P(('groups', 'expert', 'sub')), parts along dimension 0
The draws below stay inside these ranges and needn't reach their ends.
There are 2 independent parts, one for each index of `groups`. The reference program is written for one: setup_inputs(seed, part) draws one part's arguments, and reference() takes and returns one part's arrays. A program takes and returns all parts, laid end to end along the dimension named above; an argument that names none is the same for every part. Nothing has to cross between parts.
Inputs may be any that keep to these rules, and one draw needn't show every extreme that they name: `routes`: each token names 4 different experts; among the 128 tokens of one device no expert is named more than 96 times, a bound that some block reaches.
All inputs are finite; a program needn't handle non-finite values.
Results may differ from the reference program's by a relative error of at most 0.0058.
Values may be sent and summed in bfloat16 or wider, within the bound.
A program may use at most 128 MiB of HBM per device.

```python
import math
import jax
import jax.numpy as jnp
import numpy as np
from jax import lax

LATENT = 1024
HIDDEN_SIZE = 2688
TOK_DEV = 128
TOPK = 4
EXPERTS = 8
MOST = 96
TOKENS = 2048


def levels(key, shape, split, least, high):
    loudness = 1.0
    for axis_at, parts in split:
        steps = jax.random.uniform(jax.random.fold_in(jax.random.fold_in(key, 6), axis_at), (parts,), jnp.float32, least / len(split), high / len(split))
        loudness = loudness * jnp.repeat(jnp.exp(steps), shape[axis_at] // parts).reshape((-1,) + (1,) * (len(shape) - 1 - axis_at))
    return loudness


def shared_out(stream_key, own, number, rows, number_of, top, limit, slope):
    order = jax.random.permutation(stream_key, number_of)
    heavy_load, ordinary = load_shares(number_of, rows * top, limit, slope, True), load_shares(number_of, rows * top, limit, slope, False)
    places = jnp.arange(number_of)

    def named(tallies, offset_by):
        used = int((tallies > 0).sum())
        fixed = max(1, used // 4)
        shifted = fixed + (places - fixed + offset_by * (used - fixed)) % max(1, number_of - fixed)
        return jnp.zeros((number_of,), jnp.int32).at[order[jnp.where(places < fixed, places, shifted)]].set(jnp.asarray(tallies, jnp.int32))

    tallies = jnp.where(number % 4 == 0, named(heavy_load, number // 4), named(ordinary, number - number // 4 - 1))
    mixed = jax.random.permutation(jax.random.fold_in(own, 3), number_of)
    donor, receiver = mixed[0:number_of // 2 * 2:2], mixed[1:number_of // 2 * 2:2]
    margin = jnp.minimum(tallies[donor] - 1, limit - tallies[receiver]) // 2
    margin = jnp.where((donor == order[0]) | (receiver == order[0]) | (tallies[receiver] == 0), 0, jnp.maximum(margin, 0))
    shifted = jax.random.randint(jax.random.fold_in(own, 4), (number_of // 2,), 0, 1 << 20) % (margin + 1)
    tallies = tallies.at[donor].add(-shifted).at[receiver].add(shifted)
    members = jnp.searchsorted(jnp.cumsum(tallies), jnp.arange(rows * top), side="right").astype(jnp.int32)
    listing = members.reshape(top, rows).T
    listing = listing[jax.random.permutation(jax.random.fold_in(own, 1), rows)]
    offset_by = jax.random.randint(jax.random.fold_in(own, 2), (rows, 1), 0, top)
    return jnp.take_along_axis(listing, (jnp.arange(top)[None, :] + offset_by) % top, axis=1)


def load_shares(amount, total, limit, lean, full):
    weights = [(1 << 20) // math.isqrt(grade ** lean) + 1 for grade in range(1, amount + 1)]
    largest = limit if full else min(limit, max(-(-total // amount), total * weights[0] // sum(weights)))
    least = 1 if total - largest >= amount - 1 else 0
    given, rest = [largest] + [least] * (amount - 1), total - largest - least * (amount - 1)
    while rest > 0:
        movable = [i for i in range(1, amount) if given[i] < largest] or [i for i in range(1, amount) if given[i] < limit]
        pool, left = sum([weights[i] for i in movable]), rest
        for i in movable:
            more = min(limit - given[i], max(1, left * weights[i] // pool), rest)
            given[i] = given[i] + more
            rest = rest - more
    return np.array(given)


def centred(key, extent, spread, reach, split=(), kind=jnp.bfloat16):
    array = spread * jax.random.normal(key, extent, jnp.float32)
    if split:
        array = array * levels(key, extent, split, -0.22, 0.18)
    return jnp.clip(array, -reach, reach).astype(kind)


def setup_inputs(seed: int = 0, part: int = 0) -> dict:
    key_of = jax.random.split(jax.random.key(seed), 6)
    part_keys = jax.random.split(jax.random.fold_in(key_of[5], part), 6)
    latent = centred(part_keys[0], (TOKENS, LATENT), 1.0, 6.0, ((0, 16),))
    routes_keys = jax.random.split(jax.random.fold_in(part_keys[1], 1), TOKENS // TOK_DEV)
    routes_turns = jax.random.permutation(jax.random.fold_in(part_keys[1], 3), TOKENS // TOK_DEV)
    routes = jax.vmap(lambda own, number: shared_out(jax.random.fold_in(part_keys[1], 2), own, number, TOK_DEV, EXPERTS, TOPK, MOST, 2))(routes_keys, routes_turns).reshape((TOKENS, TOPK))
    gates = jnp.clip(0.1 + 0.9 * jax.random.uniform(part_keys[2], (TOKENS, TOPK), jnp.float32) ** levels(part_keys[2], (TOKENS, TOPK), ((0, 16),), -0.2, 0.2), 0.1, 1.0)
    up_weight = centred(key_of[3], (EXPERTS, LATENT, HIDDEN_SIZE), LATENT ** -0.5, 0.1875, ((0, 8), (2, 2)))
    down_weight = centred(key_of[4], (EXPERTS, LATENT, HIDDEN_SIZE), HIDDEN_SIZE ** -0.5, 0.125, ((0, 8), (2, 2)))
    return dict(latent=latent, routes=routes, gates=gates, up_weight=up_weight, down_weight=down_weight)


def expert_rows(gathered, up_part, down_part):
    preact = jnp.dot(gathered, up_part, preferred_element_type=jnp.float32)
    active = jnp.square(jnp.maximum(preact, 0.0)).astype(jnp.bfloat16)
    return lax.dot_general(active, down_part, (((1,), (1,)), ((), ())), preferred_element_type=jnp.float32)


def reference(latent, routes, gates, up_weight, down_weight):
    pair_count = TOKENS * TOPK
    route_ids = routes.reshape(-1).astype(jnp.int32)
    tok_index = jnp.arange(pair_count, dtype=jnp.int32) // TOPK
    flat_gate = gates.reshape(-1)
    padded = jnp.concatenate([latent, jnp.zeros((1, LATENT), latent.dtype)], axis=0)
    capacity = (TOKENS // TOK_DEV) * MOST

    def one_expert(carry, expert):
        chosen = jnp.nonzero(route_ids == expert, size=capacity, fill_value=pair_count)[0].astype(jnp.int32)
        is_live = chosen < pair_count
        clipped = jnp.minimum(chosen, pair_count - 1).astype(jnp.int32)
        token_of = jnp.where(is_live, tok_index[clipped], TOKENS).astype(jnp.int32)
        gathered = padded[token_of]
        rounded = expert_rows(gathered, up_weight[expert], down_weight[expert]).astype(jnp.bfloat16)
        rounded = lax.optimization_barrier(rounded).astype(jnp.float32)
        weight = jnp.where(is_live, flat_gate[clipped], jnp.float32(0.0))
        carry = carry.at[token_of].add(weight[:, None] * rounded)
        return carry, None

    summed = lax.scan(one_expert, jnp.zeros((TOKENS + 1, LATENT), jnp.float32), jnp.arange(EXPERTS, dtype=jnp.int32))[0]
    return summed[:TOKENS].astype(jnp.bfloat16)
```

```python
import jax
import jax.numpy as jnp
from jax import lax
from jax.experimental import pallas as pl
from jax.experimental.pallas import tpu as pltpu
from jax.sharding import PartitionSpec as P

CORES = 2
PIECES = 4
VMEM_MOST = 60 * 1024 * 1024
F32, BF16 = jnp.float32, jnp.bfloat16


END_UNITS = (
    (0, 1, 2, 3),
    (4, 5, 17, 18),
    (21, 8, 6, 16),
    (20, 24, 12, 10),
    (25, 28, 14, 19),
    (26, 29, 30, 31),
    (22, 27, 13, 15),
    (23, 9, 11, 7),
)
END_MOVES = (
    (
        (0, 0), (0, 1), (0, 2), (0, 3), (1, 0, 1, 1), (1, 2, 1, 1), (1, 1, 0, 4), (1, 2, 0, 4), (1, 3, 1, 1),
        (1, 0, 0, 4), (1, 1, 1, 1),
    ),
    (
        (0, 5), (0, 17), (0, 4), (0, 18), (1, 17, 1, 5), (1, 5, 0, 5), (1, 3, 0, 4), (1, 18, 1, 5), (0, 6),
        (0, 16),
    ),
    (
        (0, 21), (0, 8), (1, 8, 0, 6), (0, 19), (0, 20), (2, 17, 0, 0, 0), (2, 4, 1, 0, 0), (2, 5, 1, 0, 0),
    ),
    (
        (0, 10), (0, 24), (0, 12), (1, 12, 0, 7), (1, 10, 0, 6), (0, 25), (2, 16, 0, 0, 0), (2, 8, 1, 3, 0),
        (2, 21, 1, 4, 0),
    ),
    (
        (0, 14), (0, 28), (1, 14, 0, 7), (0, 15), (0, 26), (2, 24, 1, 7, 0), (2, 20, 1, 4, 0), (0, 29),
    ),
    (
        (0, 31), (0, 30), (0, 11), (1, 11, 0, 6), (2, 28, 0, 3, 0), (2, 14, 1, 2, 0), (2, 25, 1, 7, 0),
    ),
    (
        (0, 13), (0, 27), (0, 22), (2, 12, 1, 2, 1), (0, 23), (2, 29, 0, 3, 0), (2, 30, 1, 6, 0),
        (2, 26, 0, 2, 0),
    ),
    (
        (0, 7), (0, 9), (2, 31, 1, 6, 0), (2, 13, 1, 2, 1), (2, 15, 1, 2, 0), (2, 27, 0, 2, 0),
        (2, 22, 0, 1, 0),
    ),
    (
        (2, 10, 1, 3, 1), (2, 9, 1, 3, 0), (2, 11, 1, 3, 1), (2, 23, 0, 1, 0), (2, 0, 3, 0, 3),
        (2, 6, 1, 0, 1), (2, 18, 0, 0, 2), (2, 7, 1, 0, 1), (2, 19, 0, 0, 2), (2, 1, 3, 0, 3),
        (2, 2, 3, 0, 3), (2, 3, 3, 0, 3),
    ),
)
INNER_UNITS = (
    (0, 1, 2, 3),
    (12, 13, 4, 6),
    (14, 16, 18, 19),
    (8, 15, 5, 7),
    (10, 21, 22, 23),
    (11, 24, 25, 20),
    (26, 27, 17, 28),
    (9, 29, 30, 31),
)
INNER_MOVES = (
    (
        (0, 0), (0, 1), (0, 2), (0, 3), (1, 0, 2, 3), (1, 1, 2, 3), (1, 1, 1, 1), (1, 0, 1, 1), (1, 0, 0, 4),
        (1, 2, 0, 4), (1, 2, 2, 3), (1, 2, 1, 1), (1, 3, 0, 4), (1, 3, 2, 3),
    ),
    (
        (0, 4), (0, 12), (0, 6), (0, 13), (0, 16), (0, 18), (1, 13, 0, 7), (1, 12, 0, 7), (1, 4, 2, 2),
        (1, 12, 1, 2), (1, 16, 1, 5), (1, 6, 2, 2), (0, 7), (0, 14), (0, 19), (1, 7, 0, 5), (1, 14, 1, 2),
    ),
    (
        (0, 15), (0, 5), (0, 21), (0, 29), (0, 8), (1, 8, 1, 3), (1, 21, 2, 6), (1, 8, 0, 6), (1, 7, 2, 2),
        (1, 29, 1, 6), (1, 4, 0, 5),
    ),
    (
        (0, 28), (0, 10), (0, 22), (0, 23), (1, 10, 1, 3), (1, 23, 2, 6), (1, 22, 2, 6), (1, 1, 0, 4),
    ),
    (
        (0, 25), (0, 24), (0, 11), (0, 20), (1, 11, 1, 3), (1, 5, 2, 2), (1, 25, 1, 7), (2, 18, 0, 0, 0),
    ),
    (
        (0, 27), (0, 26), (0, 17), (1, 27, 1, 7), (1, 15, 1, 2), (1, 18, 2, 7), (1, 19, 2, 7),
    ),
    (
        (0, 9), (1, 9, 1, 3), (2, 12, 2, 0, 2), (2, 21, 0, 1, 0),
    ),
    (
        (0, 30), (0, 31), (1, 18, 1, 5), (1, 19, 1, 5), (2, 24, 2, 5, 0), (2, 25, 0, 2, 0), (1, 3, 1, 1),
        (2, 28, 2, 4, 2), (2, 17, 0, 0, 2),
    ),
    (
        (2, 20, 0, 1, 4), (2, 10, 2, 1, 2), (1, 13, 1, 2), (2, 16, 0, 0, 6), (2, 30, 0, 3, 0),
        (2, 31, 2, 4, 0), (2, 29, 0, 3, 2), (2, 6, 1, 0, 4), (2, 8, 2, 1, 2), (2, 0, 3, 0, 7),
        (2, 19, 0, 0, 4), (2, 26, 2, 5, 2), (2, 27, 2, 5, 2), (2, 4, 1, 0, 5), (2, 9, 2, 1, 3),
        (2, 22, 1, 4, 4), (2, 11, 2, 1, 2), (2, 23, 1, 4, 4), (2, 14, 2, 0, 3), (2, 5, 1, 0, 5),
        (2, 13, 2, 0, 3), (2, 7, 1, 0, 4), (2, 15, 2, 0, 2), (2, 2, 3, 0, 7), (2, 1, 3, 0, 7),
        (2, 3, 3, 0, 7),
    ),
)


def expert_part(row_block, up_part, down_part):
    preact = jnp.dot(row_block, up_part, preferred_element_type=F32)
    active = jnp.square(jnp.maximum(preact, 0.0)).astype(BF16)
    return lax.dot_general(
        active, down_part, (((1,), (1,)), ((), ())), preferred_element_type=F32
    )


def routed(latent, routes, gates, up_weight, down_weight):
    tokens_here, row_width = latent.shape
    top_count = routes.shape[1]
    experts = lax.axis_size("expert")
    slot_most = min(tokens_here, 3 * tokens_here * top_count // (2 * experts))
    pair_count = tokens_here * top_count
    route_ids = routes.reshape(-1)
    one_hot = (route_ids[:, None] == jnp.arange(experts, dtype=jnp.int32)[None, :]).astype(
        jnp.int32
    )
    before = jnp.cumsum(one_hot, axis=0) - one_hot
    slot_rank = jnp.sum(before * one_hot, axis=1)
    slot_of = route_ids * slot_most + slot_rank
    source = (
        jnp.full((experts * slot_most,), pair_count, jnp.int32)
        .at[slot_of]
        .set(jnp.arange(pair_count, dtype=jnp.int32))
    )
    padded = jnp.concatenate([latent, jnp.zeros((1, row_width), latent.dtype)], axis=0)
    send_rows = padded[source // top_count].reshape(experts, slot_most, row_width)
    arrived = lax.all_to_all(send_rows, "expert", split_axis=0, concat_axis=0, tiled=True)
    flat_rows = arrived.reshape(-1, row_width)
    summed = expert_part(
        flat_rows,
        lax.all_gather(up_weight, "sub", axis=2, tiled=True)[0],
        lax.all_gather(down_weight, "sub", axis=2, tiled=True)[0],
    )
    expert_out = lax.all_to_all(
        summed.astype(BF16).reshape(arrived.shape),
        "expert",
        split_axis=0,
        concat_axis=0,
        tiled=True,
    )
    values = expert_out.reshape(experts * slot_most, row_width)[slot_of].astype(F32)
    mixed_out = jnp.sum(
        values.reshape(tokens_here, top_count, row_width) * gates[:, :, None], axis=1
    )
    return mixed_out.astype(BF16)


def grid_kernel(
    routes_hbm, gates_hbm, latent_hbm, up_hbm, down_hbm, out_ref,
    routes, gates, mine, tables, rows, up, down, kept, mate_out, mate_in, sums_out, sums_in,
    small_sem, own_sem, w_sem, table_s, table_r, cross_s, cross_r,
    near_s, near_r, far_s, far_r, mate_s, mate_r, sum_s, sum_r,
):
    me = lax.axis_index("expert")
    sub = lax.axis_index("sub")
    chip, core = me // CORES, me % CORES
    lanes = tables.shape[1]
    experts = mine.shape[0]
    part = rows.shape[2]
    inner = ((chip + 1) // 2) % 2 == 1

    def place(step):
        first = (chip + step) % 2
        second = (chip // 2 + step // 2) % 2
        return first + 2 * second

    sibling = {"expert": chip * CORES + 1 - core}
    roads = ({"sub": 1 - sub}, {"expert": place(1) * CORES + core}, {"expert": place(3) * CORES + core})

    def send(src, dst, s_sem, r_sem, device):
        return pltpu.make_async_remote_copy(
            src_ref=src, dst_ref=dst, send_sem=s_sem, recv_sem=r_sem,
            device_id=device, device_id_type=pl.DeviceIdType.MESH,
        )

    small = [
        pltpu.make_async_copy(routes_hbm, routes, small_sem.at[0]),
        pltpu.make_async_copy(gates_hbm, gates, small_sem.at[1]),
    ]
    own = [
        pltpu.make_async_copy(latent_hbm.at[pl.ds(piece * part, part)], rows.at[piece, 0], own_sem.at[piece])
        for piece in range(PIECES)
    ]
    weights = [
        pltpu.make_async_copy(up_hbm.at[0], up, w_sem.at[0]),
        pltpu.make_async_copy(down_hbm.at[0], down, w_sem.at[1]),
    ]
    for copy in (*own, *small, *weights):
        copy.start()

    column = [
        (step, side) for step in range(lanes) for side in range(CORES) if step or side
    ]

    def table_peer(step, side):
        return place(step) * CORES + (core + side) % CORES

    barrier = pltpu.get_barrier_semaphore()
    greeted = [roads[0]] + [{"expert": table_peer(*who)} for who in column]
    for device in greeted:
        pl.semaphore_signal(barrier, inc=1, device_id=device, device_id_type=pl.DeviceIdType.MESH)
    for copy in (*small, *own):
        copy.wait()
    for expert in range(experts):
        mine[expert] = jnp.sum(
            jnp.where(routes[...] == expert, gates[...], 0.0), axis=0, keepdims=True
        )
    tables[0, 0, 0] = mine[me]
    pl.semaphore_wait(barrier, len(greeted))

    def to_column(step, side):
        return send(mine.at[table_peer(step, side)], tables.at[0, step, side], table_s,
                    table_r.at[step * CORES + side], {"expert": table_peer(step, side)})

    across = send(tables.at[0], tables.at[1], cross_s, cross_r, roads[0])

    def to_mate(code):
        return send(rows.at[code, 0], rows.at[code, 1], near_s, near_r.at[code], sibling)

    def onward(code, road, block):
        spot = block * PIECES + code % PIECES
        return send(rows.at[code, 0], rows.at[spot, 0], far_s, far_r.at[spot], roads[road])

    def part_to_mate(unit):
        return send(mate_out.at[unit], mate_in.at[unit], mate_s, mate_r.at[unit], sibling)

    def sum_onward(code, road, block):
        spot = block * PIECES + code % PIECES
        return send(sums_out.at[code], sums_in.at[3 * spot + road], sum_s, sum_r.at[spot, road], roads[road])

    def landed(code):
        onward(code, 0, code // PIECES).wait_recv()

    def run(units, phase, seen, joined):
        for move in phase:
            code = move[1]
            if move[0] < 2:
                if code >= PIECES and code not in seen:
                    landed(code)
                    seen.add(code)
                if move[0] == 0:
                    to_mate(code).start()
                else:
                    onward(code, move[2], move[3]).start()
                continue
            unit = [code in group for group in units].index(True)
            spot = units[unit].index(code)
            if unit not in joined:
                part_to_mate(unit).wait_recv()
                joined.add(unit)
            total = kept[unit, spot] + mate_in[unit, spot].astype(F32)
            for road in range(len(roads)):
                if move[4] >> road & 1:
                    sum_r_of = send(sums_out.at[code], sums_in.at[3 * code + road], sum_s,
                                    sum_r.at[code, road], roads[road])
                    sum_r_of.wait_recv()
                    total = total + sums_in[3 * code + road].astype(F32)
            if move[2] < len(roads):
                sums_out[code] = total.astype(BF16)
                sum_onward(code, *move[2:4]).start()
            else:
                out_ref[pl.ds(code * part, part)] = total.astype(BF16)

    plans = ((END_UNITS, END_MOVES), (INNER_UNITS, INNER_MOVES))
    known = ((set(), set()), (set(), set()))

    def both(phase, index):
        for role in (0, 1):
            @pl.when(inner == (role == 1))
            def _():
                units, moves = plans[role]
                run(units, moves[phase], *known[role])
                if phase < len(units):
                    for code in units[phase]:
                        to_mate(code).wait_recv()

    count = len(END_UNITS)
    width = len(END_UNITS[0])

    def lookup(index, spot):
        code = 0
        for unit in range(count):
            here = jnp.where(inner, INNER_UNITS[unit][spot], END_UNITS[unit][spot])
            code = jnp.where(index == unit, here, code)
        return code

    def gate_column(code, side):
        block, piece = code // PIECES, code % PIECES
        line = tables[block // lanes, block % lanes, side]
        row = lax.broadcasted_iota(jnp.int32, (part, line.shape[1]), 0) + piece * part
        lane = lax.broadcasted_iota(jnp.int32, (part, line.shape[1]), 1)
        return jnp.sum(jnp.where(row == lane, line, 0.0), axis=1, keepdims=True)

    def one(index, carry):
        for phase in range(count):
            @pl.when(index == phase)
            def _():
                if phase == 0:
                    for who in column:
                        to_column(*who).start()
                both(phase, index)
                if phase == 0:
                    for who in column:
                        to_column(*who).wait_recv()
                    across.start()
                    for copy in weights:
                        copy.wait()
                    across.wait_recv()

        codes = [lookup(index, spot) for spot in range(width)]
        block = jnp.concatenate([rows[code, side] for side in (0, 1) for code in codes], axis=0)
        preact = lax.dot_general(
            block, up[...], (((1,), (1,)), ((), ())), preferred_element_type=F32
        )
        active = jnp.square(jnp.maximum(preact, 0.0)).astype(BF16)
        result = jnp.dot(active, down[...], preferred_element_type=F32)
        for spot, code in enumerate(codes):
            near = result[spot * part:(spot + 1) * part]
            away = result[(width + spot) * part:(width + spot + 1) * part]
            kept[index, spot] = near * gate_column(code, 0)
            mate_out[index, spot] = (away * gate_column(code, 1)).astype(BF16)
        part_to_mate(index).start()
        return carry

    lax.fori_loop(0, count, one, 0)
    both(count, count)

    for who in column:
        to_column(*who).wait_send()
    across.wait_send()
    send(mate_out, mate_in, near_s, near_s, sibling).wait_send()
    send(mate_out, mate_in, mate_s, mate_s, sibling).wait_send()
    for role in (0, 1):
        @pl.when(inner == (role == 1))
        def _():
            moves = [move for phase in plans[role][1] for move in phase]
            for kind, sem in ((1, far_s), (2, sum_s)):
                sent = sum(move[0] == kind and move[2] < len(roads) for move in moves)
                whole = sums_in.at[pl.ds(0, sent)]
                send(whole, whole, sem, sem, roads[0]).wait_send()


def grid(latent, routes, gates, up_weight, down_weight):
    tokens, width = latent.shape
    top_count = routes.shape[1]
    hidden = up_weight.shape[2]
    experts = lax.axis_size("expert")
    lanes = experts // CORES
    blocks, part = 2 * lanes, tokens // PIECES
    units, spots = len(END_UNITS), len(END_UNITS[0])
    vmem = pl.BlockSpec(memory_space=pltpu.VMEM)
    hbm = pl.BlockSpec(memory_space=pl.ANY)
    dma = pltpu.SemaphoreType.DMA
    return pl.pallas_call(
        grid_kernel,
        out_shape=jax.ShapeDtypeStruct((tokens, width), BF16),
        in_specs=[hbm] * 5,
        out_specs=vmem,
        scratch_shapes=[
            pltpu.VMEM((top_count, tokens), jnp.int32),
            pltpu.VMEM((top_count, tokens), F32),
            pltpu.VMEM((experts, 1, tokens), F32),
            pltpu.VMEM((2, lanes, CORES, 1, tokens), F32),
            pltpu.VMEM((blocks * PIECES, 2, part, width), BF16),
            pltpu.VMEM((hidden, width), BF16),
            pltpu.VMEM((hidden, width), BF16),
            pltpu.VMEM((units, spots, part, width), F32),
            pltpu.VMEM((units, spots, part, width), BF16),
            pltpu.VMEM((units, spots, part, width), BF16),
            pltpu.VMEM((blocks * PIECES, part, width), BF16),
            pltpu.VMEM((blocks * PIECES * 3, part, width), BF16),
            dma((2,)), dma((PIECES,)), dma((2,)),
            dma, dma((lanes * CORES,)), dma, dma,
            dma, dma((blocks * PIECES,)), dma, dma((blocks * PIECES,)),
            dma, dma((units,)), dma, dma((blocks * PIECES, 3)),
        ],
        compiler_params=pltpu.CompilerParams(
            collective_id=0, has_side_effects=True, vmem_limit_bytes=VMEM_MOST
        ),
    )(routes.T, gates.T, latent, jnp.swapaxes(up_weight, 1, 2), jnp.swapaxes(down_weight, 1, 2))


def local(latent, routes, gates, up_weight, down_weight):
    tokens, width = latent.shape
    experts, subs = lax.axis_size("expert"), lax.axis_size("sub")
    block = tokens * width * 2
    need = 8 * block * (2 + 2 + 1 + 1 + 1 + 3) + 4 * up_weight.size + 4 * block
    fits = subs == 2 and experts == 4 * CORES and need < VMEM_MOST
    plan = grid if fits and tokens % (16 * PIECES) == 0 and tokens % 128 == 0 else routed
    return plan(latent, routes, gates, up_weight, down_weight)


def solution(mesh):
    placed = (
        P(("groups", "expert", "sub"), None),
        P(("groups", "expert", "sub"), None),
        P(("groups", "expert", "sub"), None),
        P("expert", None, "sub"),
        P("expert", None, "sub"),
    )
    return jax.shard_map(
        local,
        mesh=mesh,
        in_specs=placed,
        out_specs=P(("groups", "expert", "sub"), None),
        check_vma=False,
    )
```

```python
import jax
import jax.numpy as jnp
from jax import lax
from jax.experimental import pallas as pl
from jax.experimental.pallas import tpu as pltpu
from jax.sharding import PartitionSpec as P

CORES = 2
PIECES = 4
ROADS = 4
VMEM_MOST = 60 * 1024 * 1024
F32, BF16 = jnp.float32, jnp.bfloat16


END_UNITS = (
    (0, 1, 2, 3),
    (18, 4, 7, 16),
    (9, 17, 19, 5),
    (13, 15, 20, 23),
    (28, 29, 25, 12),
    (30, 31, 24, 27),
    (26, 14, 11, 22),
    (8, 21, 10, 6),
)
END_MOVES = (
    (
        (0, 0), (0, 1), (0, 2), (0, 3), (1, 2, 1, 1), (1, 2, 0, 4), (1, 0, 3, 2), (1, 0, 0, 4), (1, 1, 3, 2),
        (1, 1, 0, 4),
    ),
    (
        (1, 3, 1, 1), (1, 3, 0, 4), (0, 18), (0, 4), (1, 3, 2, 3), (1, 4, 0, 5), (0, 16), (0, 7),
        (1, 1, 1, 1), (1, 7, 0, 5),
    ),
    (
        (0, 17), (0, 5), (0, 19), (0, 9), (1, 9, 0, 6), (1, 2, 3, 2), (1, 16, 1, 5), (0, 20), (1, 0, 1, 1),
        (2, 18, 0, 0, 0),
    ),
    (
        (0, 15), (0, 23), (0, 13), (0, 25), (1, 13, 0, 7), (1, 15, 0, 7), (2, 7, 1, 0, 0), (0, 12),
        (2, 9, 1, 3, 0), (2, 17, 0, 0, 0),
    ),
    (
        (0, 11), (0, 28), (0, 29), (1, 11, 0, 6), (0, 31), (0, 24), (2, 13, 1, 2, 0), (2, 15, 1, 2, 0),
        (2, 20, 0, 1, 0),
    ),
    (
        (0, 30), (0, 27), (2, 23, 1, 4, 0), (0, 14), (2, 28, 0, 3, 0), (2, 29, 1, 6, 0), (2, 25, 1, 7, 0),
    ),
    (
        (0, 26), (0, 22), (2, 4, 1, 0, 1), (0, 8), (2, 12, 1, 2, 1), (2, 30, 0, 3, 0), (2, 24, 0, 2, 0),
        (2, 31, 1, 6, 0),
    ),
    (
        (0, 21), (0, 10), (2, 27, 0, 2, 0), (0, 6), (2, 14, 1, 2, 1), (2, 26, 0, 2, 0), (2, 22, 0, 1, 0),
    ),
    (
        (2, 11, 3, 0, 1), (2, 19, 0, 0, 2), (2, 10, 1, 3, 1), (2, 8, 1, 3, 1), (2, 21, 0, 1, 0),
        (2, 16, 0, 0, 2), (2, 6, 1, 0, 1), (2, 5, 1, 0, 1), (2, 1, 4, 0, 3), (2, 0, 4, 0, 3),
        (2, 3, 4, 0, 11), (2, 2, 4, 0, 3),
    ),
)
INNER_UNITS = (
    (0, 2, 3, 1),
    (18, 16, 6, 13),
    (8, 9, 17, 7),
    (22, 19, 5, 15),
    (11, 28, 23, 24),
    (10, 31, 25, 26),
    (20, 21, 4, 14),
    (29, 27, 12, 30),
)
INNER_MOVES = (
    (
        (0, 0), (0, 1), (0, 2), (0, 3), (1, 0, 0, 4), (1, 2, 0, 4), (1, 1, 2, 3), (1, 0, 1, 1), (1, 3, 1, 1),
        (1, 1, 0, 4), (1, 1, 1, 1),
    ),
    (
        (1, 3, 2, 3), (0, 16), (0, 6), (0, 13), (1, 13, 1, 2), (1, 6, 0, 5), (1, 3, 0, 4), (0, 18), (0, 8),
        (1, 8, 0, 6), (1, 16, 2, 7),
    ),
    (
        (0, 9), (0, 17), (0, 7), (0, 22), (1, 7, 2, 2), (1, 9, 1, 3), (1, 8, 1, 3), (1, 9, 0, 6),
        (1, 7, 0, 5), (0, 15), (0, 19), (1, 15, 1, 2), (1, 15, 0, 7),
    ),
    (
        (0, 5), (0, 24), (0, 28), (0, 25), (1, 22, 2, 6), (1, 24, 1, 7), (1, 18, 2, 7), (1, 28, 1, 6),
        (2, 18, 0, 0, 0), (1, 5, 0, 5), (0, 11), (1, 2, 2, 3), (0, 23), (0, 20),
    ),
    (
        (0, 10), (0, 31), (0, 4), (0, 26), (1, 26, 1, 7), (1, 10, 1, 3), (1, 0, 2, 3), (1, 11, 0, 6),
    ),
    (
        (0, 30), (0, 21), (1, 30, 1, 6), (2, 22, 0, 1, 0), (1, 18, 1, 5), (1, 17, 2, 7), (2, 13, 2, 0, 2),
        (0, 14),
    ),
    (
        (0, 12), (0, 27), (2, 28, 2, 4, 0), (2, 24, 0, 2, 0), (1, 12, 1, 2), (1, 17, 1, 5),
    ),
    (
        (0, 29), (2, 26, 0, 2, 0), (1, 14, 1, 2), (2, 31, 0, 3, 0), (2, 9, 2, 1, 2), (1, 2, 1, 1),
        (2, 19, 0, 0, 2),
    ),
    (
        (2, 25, 2, 5, 2), (2, 16, 0, 0, 4), (2, 7, 1, 0, 0), (2, 23, 1, 4, 0), (2, 29, 2, 4, 2),
        (2, 30, 0, 3, 0), (2, 15, 2, 0, 1), (2, 20, 1, 4, 0), (2, 8, 2, 1, 3), (2, 21, 0, 1, 4),
        (2, 27, 0, 2, 2), (2, 17, 0, 0, 4), (2, 10, 2, 1, 3), (2, 5, 1, 0, 5), (2, 4, 1, 0, 4),
        (2, 11, 3, 0, 3), (2, 3, 4, 0, 15), (2, 14, 2, 0, 3), (2, 6, 1, 0, 5), (2, 12, 2, 0, 2),
        (2, 2, 4, 0, 7), (2, 1, 4, 0, 7), (2, 0, 4, 0, 7),
    ),
)


def expert_part(row_block, up_part, down_part):
    preact = jnp.dot(row_block, up_part, preferred_element_type=F32)
    active = jnp.square(jnp.maximum(preact, 0.0)).astype(BF16)
    return lax.dot_general(
        active, down_part, (((1,), (1,)), ((), ())), preferred_element_type=F32
    )


def routed(latent, routes, gates, up_weight, down_weight):
    tokens_here, row_width = latent.shape
    top_count = routes.shape[1]
    experts = lax.axis_size("expert")
    slot_most = min(tokens_here, 3 * tokens_here * top_count // (2 * experts))
    pair_count = tokens_here * top_count
    route_ids = routes.reshape(-1)
    one_hot = (route_ids[:, None] == jnp.arange(experts, dtype=jnp.int32)[None, :]).astype(
        jnp.int32
    )
    before = jnp.cumsum(one_hot, axis=0) - one_hot
    slot_rank = jnp.sum(before * one_hot, axis=1)
    slot_of = route_ids * slot_most + slot_rank
    source = (
        jnp.full((experts * slot_most,), pair_count, jnp.int32)
        .at[slot_of]
        .set(jnp.arange(pair_count, dtype=jnp.int32))
    )
    padded = jnp.concatenate([latent, jnp.zeros((1, row_width), latent.dtype)], axis=0)
    send_rows = padded[source // top_count].reshape(experts, slot_most, row_width)
    arrived = lax.all_to_all(send_rows, "expert", split_axis=0, concat_axis=0, tiled=True)
    flat_rows = arrived.reshape(-1, row_width)
    summed = expert_part(
        flat_rows,
        lax.all_gather(up_weight, "sub", axis=2, tiled=True)[0],
        lax.all_gather(down_weight, "sub", axis=2, tiled=True)[0],
    )
    expert_out = lax.all_to_all(
        summed.astype(BF16).reshape(arrived.shape),
        "expert",
        split_axis=0,
        concat_axis=0,
        tiled=True,
    )
    values = expert_out.reshape(experts * slot_most, row_width)[slot_of].astype(F32)
    mixed_out = jnp.sum(
        values.reshape(tokens_here, top_count, row_width) * gates[:, :, None], axis=1
    )
    return mixed_out.astype(BF16)


def grid_kernel(
    routes_hbm, gates_hbm, latent_hbm, up_hbm, down_hbm, out_ref,
    routes, gates, mine, tables, rows, up, down, kept, mate_out, mate_in, sums_out, sums_in,
    small_sem, own_sem, w_sem, table_s, table_r, cross_s, cross_r,
    near_s, near_r, far_s, far_r, mate_s, mate_r, sum_s, sum_r,
):
    me = lax.axis_index("expert")
    sub = lax.axis_index("sub")
    chip, core = me // CORES, me % CORES
    lanes = tables.shape[1]
    experts = mine.shape[0]
    part = rows.shape[2]
    inner = ((chip + 1) // 2) % 2 == 1

    def place(step):
        first = (chip + step) % 2
        second = (chip // 2 + step // 2) % 2
        return first + 2 * second

    sibling = {"expert": chip * CORES + 1 - core}
    roads = ({"sub": 1 - sub},) + tuple(
        {"expert": place(step) * CORES + core} for step in (1, 3, 2)
    )

    def send(src, dst, s_sem, r_sem, device):
        return pltpu.make_async_remote_copy(
            src_ref=src, dst_ref=dst, send_sem=s_sem, recv_sem=r_sem,
            device_id=device, device_id_type=pl.DeviceIdType.MESH,
        )

    small = [
        pltpu.make_async_copy(routes_hbm, routes, small_sem.at[0]),
        pltpu.make_async_copy(gates_hbm, gates, small_sem.at[1]),
    ]
    own = [
        pltpu.make_async_copy(latent_hbm.at[pl.ds(piece * part, part)], rows.at[piece, 0], own_sem.at[piece])
        for piece in range(PIECES)
    ]
    weights = [
        pltpu.make_async_copy(up_hbm.at[0], up, w_sem.at[0]),
        pltpu.make_async_copy(down_hbm.at[0], down, w_sem.at[1]),
    ]
    for copy in (*own, *small, *weights):
        copy.start()

    column = [
        (step, side) for step in range(lanes) for side in range(CORES) if step or side
    ]

    def table_peer(step, side):
        return place(step) * CORES + (core + side) % CORES

    barrier = pltpu.get_barrier_semaphore()
    greeted = [roads[0]] + [{"expert": table_peer(*who)} for who in column]
    for device in greeted:
        pl.semaphore_signal(barrier, inc=1, device_id=device, device_id_type=pl.DeviceIdType.MESH)
    for copy in (*small, *own):
        copy.wait()
    for expert in range(experts):
        mine[expert] = jnp.sum(
            jnp.where(routes[...] == expert, gates[...], 0.0), axis=0, keepdims=True
        )
    tables[0, 0, 0] = mine[me]
    pl.semaphore_wait(barrier, len(greeted))

    def to_column(step, side):
        return send(mine.at[table_peer(step, side)], tables.at[0, step, side], table_s,
                    table_r.at[step * CORES + side], {"expert": table_peer(step, side)})

    across = send(tables.at[0], tables.at[1], cross_s, cross_r, roads[0])

    def to_mate(code):
        return send(rows.at[code, 0], rows.at[code, 1], near_s, near_r.at[code], sibling)

    def onward(code, road, block):
        spot = block * PIECES + code % PIECES
        return send(rows.at[code, 0], rows.at[spot, 0], far_s, far_r.at[spot], roads[road])

    def part_to_mate(unit):
        return send(mate_out.at[unit], mate_in.at[unit], mate_s, mate_r.at[unit], sibling)

    def sum_onward(code, road, block):
        spot = block * PIECES + code % PIECES
        return send(sums_out.at[code], sums_in.at[ROADS * spot + road], sum_s, sum_r.at[spot, road], roads[road])

    def landed(code):
        onward(code, 0, code // PIECES).wait_recv()

    def run(units, phase, seen, joined):
        for move in phase:
            code = move[1]
            if move[0] < 2:
                if code >= PIECES and code not in seen:
                    landed(code)
                    seen.add(code)
                if move[0] == 0:
                    to_mate(code).start()
                else:
                    onward(code, move[2], move[3]).start()
                continue
            unit = [code in group for group in units].index(True)
            spot = units[unit].index(code)
            if unit not in joined:
                part_to_mate(unit).wait_recv()
                joined.add(unit)
            total = kept[unit, spot] + mate_in[unit, spot].astype(F32)
            for road in range(ROADS):
                if move[4] >> road & 1:
                    sum_r_of = send(sums_out.at[code], sums_in.at[ROADS * code + road], sum_s,
                                    sum_r.at[code, road], roads[road])
                    sum_r_of.wait_recv()
                    total = total + sums_in[ROADS * code + road].astype(F32)
            if move[2] < ROADS:
                sums_out[code] = total.astype(BF16)
                sum_onward(code, *move[2:4]).start()
            else:
                out_ref[pl.ds(code * part, part)] = total.astype(BF16)

    plans = ((END_UNITS, END_MOVES), (INNER_UNITS, INNER_MOVES))
    known = ((set(), set()), (set(), set()))

    def both(phase, index):
        for role in (0, 1):
            @pl.when(inner == (role == 1))
            def _():
                units, moves = plans[role]
                run(units, moves[phase], *known[role])
                if phase < len(units):
                    for code in units[phase]:
                        to_mate(code).wait_recv()

    count = len(END_UNITS)
    width = len(END_UNITS[0])

    def lookup(index, spot):
        code = 0
        for unit in range(count):
            here = jnp.where(inner, INNER_UNITS[unit][spot], END_UNITS[unit][spot])
            code = jnp.where(index == unit, here, code)
        return code

    def gate_column(code, side):
        block, piece = code // PIECES, code % PIECES
        line = tables[block // lanes, block % lanes, side]
        row = lax.broadcasted_iota(jnp.int32, (part, line.shape[1]), 0) + piece * part
        lane = lax.broadcasted_iota(jnp.int32, (part, line.shape[1]), 1)
        return jnp.sum(jnp.where(row == lane, line, 0.0), axis=1, keepdims=True)

    def one(index, carry):
        for phase in range(count):
            @pl.when(index == phase)
            def _():
                if phase == 0:
                    for who in column:
                        to_column(*who).start()
                both(phase, index)
                if phase == 0:
                    for who in column:
                        to_column(*who).wait_recv()
                    across.start()
                    for copy in weights:
                        copy.wait()
                    across.wait_recv()

        codes = [lookup(index, spot) for spot in range(width)]
        block = jnp.concatenate([rows[code, side] for side in (0, 1) for code in codes], axis=0)
        preact = lax.dot_general(
            block, up[...], (((1,), (1,)), ((), ())), preferred_element_type=F32
        )
        active = jnp.square(jnp.maximum(preact, 0.0)).astype(BF16)
        result = jnp.dot(active, down[...], preferred_element_type=F32)
        for spot, code in enumerate(codes):
            near = result[spot * part:(spot + 1) * part]
            away = result[(width + spot) * part:(width + spot + 1) * part]
            kept[index, spot] = near * gate_column(code, 0)
            mate_out[index, spot] = (away * gate_column(code, 1)).astype(BF16)
        part_to_mate(index).start()
        return carry

    lax.fori_loop(0, count, one, 0)
    both(count, count)

    for who in column:
        to_column(*who).wait_send()
    across.wait_send()
    send(mate_out, mate_in, near_s, near_s, sibling).wait_send()
    send(mate_out, mate_in, mate_s, mate_s, sibling).wait_send()
    for role in (0, 1):
        @pl.when(inner == (role == 1))
        def _():
            moves = [move for phase in plans[role][1] for move in phase]
            for kind, sem in ((1, far_s), (2, sum_s)):
                sent = sum(move[0] == kind and move[2] < ROADS for move in moves)
                whole = sums_in.at[pl.ds(0, sent)]
                send(whole, whole, sem, sem, roads[0]).wait_send()


def grid(latent, routes, gates, up_weight, down_weight):
    tokens, width = latent.shape
    top_count = routes.shape[1]
    hidden = up_weight.shape[2]
    experts = lax.axis_size("expert")
    lanes = experts // CORES
    blocks, part = 2 * lanes, tokens // PIECES
    units, spots = len(END_UNITS), len(END_UNITS[0])
    vmem = pl.BlockSpec(memory_space=pltpu.VMEM)
    hbm = pl.BlockSpec(memory_space=pl.ANY)
    dma = pltpu.SemaphoreType.DMA
    return pl.pallas_call(
        grid_kernel,
        out_shape=jax.ShapeDtypeStruct((tokens, width), BF16),
        in_specs=[hbm] * 5,
        out_specs=vmem,
        scratch_shapes=[
            pltpu.VMEM((top_count, tokens), jnp.int32),
            pltpu.VMEM((top_count, tokens), F32),
            pltpu.VMEM((experts, 1, tokens), F32),
            pltpu.VMEM((2, lanes, CORES, 1, tokens), F32),
            pltpu.VMEM((blocks * PIECES, 2, part, width), BF16),
            pltpu.VMEM((hidden, width), BF16),
            pltpu.VMEM((hidden, width), BF16),
            pltpu.VMEM((units, spots, part, width), F32),
            pltpu.VMEM((units, spots, part, width), BF16),
            pltpu.VMEM((units, spots, part, width), BF16),
            pltpu.VMEM((blocks * PIECES, part, width), BF16),
            pltpu.VMEM((blocks * PIECES * ROADS, part, width), BF16),
            dma((2,)), dma((PIECES,)), dma((2,)),
            dma, dma((lanes * CORES,)), dma, dma,
            dma, dma((blocks * PIECES,)), dma, dma((blocks * PIECES,)),
            dma, dma((units,)), dma, dma((blocks * PIECES, ROADS)),
        ],
        compiler_params=pltpu.CompilerParams(
            collective_id=0, has_side_effects=True, vmem_limit_bytes=VMEM_MOST
        ),
    )(routes.T, gates.T, latent, jnp.swapaxes(up_weight, 1, 2), jnp.swapaxes(down_weight, 1, 2))


def local(latent, routes, gates, up_weight, down_weight):
    tokens, width = latent.shape
    experts, subs = lax.axis_size("expert"), lax.axis_size("sub")
    block = tokens * width * 2
    need = 8 * block * (2 + 2 + 1 + 1 + 1 + ROADS) + 4 * up_weight.size + 4 * block
    fits = subs == 2 and experts == 4 * CORES and need < VMEM_MOST
    plan = grid if fits and tokens % (16 * PIECES) == 0 and tokens % 128 == 0 else routed
    return plan(latent, routes, gates, up_weight, down_weight)


def solution(mesh):
    placed = (
        P(("groups", "expert", "sub"), None),
        P(("groups", "expert", "sub"), None),
        P(("groups", "expert", "sub"), None),
        P("expert", None, "sub"),
        P("expert", None, "sub"),
    )
    return jax.shard_map(
        local,
        mesh=mesh,
        in_specs=placed,
        out_specs=P(("groups", "expert", "sub"), None),
        check_vma=False,
    )
```
